128 devices in a mesh: lat: 8 (over y_lo, z), lon: 16 (over x, y_hi, core).
Axes of the slice: x: 4, y: 4 (y_hi: 2, y_lo: 2; y = y_hi * 2 + y_lo), z: 4, core: 2. Of those that a mesh axis runs over, the one named last changes fastest.
Arguments:
- tracer: float32 [128, 3600, 128], P('lat', 'lon'), may hold values from -6 to 6
- east_courant: float32 [128, 3600, 128], P('lat', 'lon'), may hold values from -0.3 to 0.3
- east_diffusion: float32 [128, 3600, 128], P('lat', 'lon'), may hold values from 0.05 to 0.2
- south_courant: float32 [128, 3600, 128], P('lat', 'lon'), may hold values from -0.3 to 0.3
- south_diffusion: float32 [128, 3600, 128], P('lat', 'lon'), may hold values from 0.05 to 0.2
- cutoff: int32 [128], replicated, may hold values from 1 to 1800, as said below
Outputs:
- advanced: float32 [128, 3600, 128], P('lat', 'lon')
The draws below stay inside these ranges and needn't reach their ends.
Inputs may be any that keep to these rules, and one draw needn't show every extreme that they name: Rows whose distance in rows from the nearer pole is 21 or more have cutoff 1800; all other rows have cutoffs below 1800, and the two rows at the poles have cutoff 1.
All inputs are finite; a program needn't handle non-finite values.
Results may differ from the reference program's by a relative error of at most 0.000098.
Values sent between devices are 32-bit elements; how exact they have to be, the bound alone decides.
No kernel may reach another device: no remote copies, remote signals or barrier semaphores. Data moves between devices by JAX's collectives and lax.ppermute only.
A program may use at most 64 MiB of HBM per device.

```python
import math
import jax
import jax.numpy as jnp

NLON = 3600
LEV = 128
SUBSTEPS = 2
NLAT = 128
POLAR = 21


def cutoff_law(key):
    places = jnp.arange(NLAT, dtype=jnp.int32)
    distance = jnp.minimum(places, NLAT - 1 - places)
    highest = NLON // 2
    spread_top = max(2, highest // POLAR) + 2
    jitter = jax.random.randint(key, (NLAT,), 0, spread_top, dtype=jnp.int32)
    ramped = distance * highest // POLAR + jitter
    inside = jnp.clip(ramped, 1, highest - 1)
    inside = jnp.where(distance == 0, 1, inside)
    return jnp.where(distance < POLAR, inside, highest).astype(jnp.int32)


def draw_cutoff(key, part):
    return cutoff_law(jax.random.fold_in(key, 7))


def draw_tracer(key, part):
    cutoffs = cutoff_law(jax.random.fold_in(key, 7))
    columns = jnp.arange(NLON, dtype=jnp.int32)
    noise_key = jax.random.fold_in(key, 11)
    phase_key = jax.random.fold_in(key, 13)
    offsets = jax.random.uniform(phase_key, (2, NLAT, 1, LEV), jnp.float32, 0.0, 2.0 * math.pi)
    step_angle = 2.0 * math.pi / NLON
    first_phase = cutoffs[:, None] * columns[None, :] % NLON
    second_phase = (11 * cutoffs // 10)[:, None] * columns[None, :] % NLON
    first_wave = jnp.cos(first_phase.astype(jnp.float32)[:, :, None] * step_angle + offsets[0])
    second_wave = jnp.cos(second_phase.astype(jnp.float32)[:, :, None] * step_angle + offsets[1])
    polar_mask = (cutoffs < NLON // 2).astype(jnp.float32)[:, None, None]
    roughness = jax.random.normal(noise_key, (NLAT, NLON, LEV), jnp.float32)
    wave_sum = 2.5 * first_wave + 1.5 * second_wave
    return jnp.clip(roughness + polar_mask * wave_sum, -6.0, 6.0).astype(jnp.float32)


def shard_levels(rng, dims, shards, smallest, top_value):
    level = 1.0
    for dim, parts in shards:
        draws = jax.random.uniform(jax.random.fold_in(jax.random.fold_in(rng, 6), dim), (parts,), jnp.float32, smallest / len(shards), top_value / len(shards))
        level = level * jnp.repeat(jnp.exp(draws), dims[dim] // parts).reshape((-1,) + (1,) * (len(dims) - 1 - dim))
    return level


def setup_inputs(seed: int = 0) -> dict:
    key_list = jax.random.split(jax.random.key(seed), 7)
    return {
        "tracer": draw_tracer(jax.random.fold_in(key_list[6], 71), 0),
        "east_courant": jnp.clip(jax.random.uniform(key_list[1], (NLAT, NLON, LEV), jnp.float32, -0.3, 0.3) * shard_levels(key_list[1], (NLAT, NLON, LEV), ((0, 8), (1, 16)), -0.4, 0.0), -0.3, 0.3),
        "east_diffusion": jnp.clip(0.05 + 0.15 * jax.random.uniform(key_list[2], (NLAT, NLON, LEV), jnp.float32) ** shard_levels(key_list[2], (NLAT, NLON, LEV), ((0, 8), (1, 16)), -0.2, 0.2), 0.05, 0.2),
        "south_courant": jnp.clip(jax.random.uniform(key_list[3], (NLAT, NLON, LEV), jnp.float32, -0.3, 0.3) * shard_levels(key_list[3], (NLAT, NLON, LEV), ((0, 8), (1, 16)), -0.4, 0.0), -0.3, 0.3),
        "south_diffusion": jnp.clip(0.05 + 0.15 * jax.random.uniform(key_list[4], (NLAT, NLON, LEV), jnp.float32) ** shard_levels(key_list[4], (NLAT, NLON, LEV), ((0, 8), (1, 16)), -0.2, 0.2), 0.05, 0.2),
        "cutoff": draw_cutoff(jax.random.fold_in(key_list[6], 71), 0),
    }


def advance(field, east_speed, east_mix, south_speed, south_mix):
    east_flux = east_speed[:, :-1] * 0.5 * (field[:, :-1] + field[:, 1:]) - east_mix[:, :-1] * (field[:, 1:] - field[:, :-1])
    south_flux = south_speed[1:] * 0.5 * (field[:-1] + field[1:]) - south_mix[1:] * (field[1:] - field[:-1])
    across = east_flux[1:-1, 1:] - east_flux[1:-1, :-1]
    meridian = south_flux[1:, 1:-1] - south_flux[:-1, 1:-1]
    return field[1:-1, 1:-1] - across - meridian


def extend_full(values):
    beside_all = jnp.concatenate([values[:, -1:], values, values[:, :1]], 1)
    return jnp.pad(beside_all, ((1, 1), (0, 0), (0, 0)))


def reference(tracer, east_courant, east_diffusion, south_courant, south_diffusion, cutoff):
    places = jnp.arange(NLAT, dtype=jnp.int32)
    keeper = (places > 0).astype(jnp.float32)[:, None, None]
    east_speed = extend_full(east_courant)
    east_mix = extend_full(east_diffusion)
    south_speed = extend_full(south_courant * keeper)
    south_mix = extend_full(south_diffusion * keeper)
    field = tracer
    for substep in range(SUBSTEPS):
        field = advance(extend_full(field), east_speed, east_mix, south_speed, south_mix)
    spectrum = jnp.fft.rfft(field, axis=1)
    waves = jnp.arange(NLON // 2 + 1).astype(jnp.float32)
    levelled = cutoff.astype(jnp.float32)[:, None]
    damping = jnp.minimum(1.0, (levelled / jnp.maximum(waves, 1.0)[None, :]) ** 2)
    smoothed = jnp.fft.irfft(spectrum * damping[:, :, None], n=NLON, axis=1).astype(jnp.float32)
    polar_rows = (cutoff < NLON // 2)[:, None, None]
    return jnp.where(polar_rows, smoothed, field)
```

```python
import functools
import math

import jax
import jax.numpy as jnp
import numpy as np
from jax import lax
from jax.experimental import pallas as pl
from jax.experimental.pallas import tpu as pltpu
from jax.sharding import PartitionSpec as P

F32 = jnp.float32
BF16 = jnp.bfloat16
CHUNKS = ((0, 80), (80, 80), (160, 65))
NP = 16
NQ = 225
BLK = 240
OUTB = 232
NK = 9


def flux(speed, mix, low, high):
    return speed * 0.5 * (low + high) - mix * (high - low)


def substep_kernel(
    f, ec, ed, sc, sd, wf, wec, wed, ef, nf, nsc, nsd, sf,
    out, first_col, last_col, first_row, last_row,
    fx, ecs, eds, scs, sds, ex, sx, ob, sem_in, sem_out,
):
    rows, cols, lanes = f.shape
    lat = lax.axis_index("lat")
    keep = jnp.where(lat > 0, 1.0, 0.0).astype(F32)

    def copies(j):
        return (
            pltpu.make_async_copy(f.at[j], fx.at[j + 1, pl.ds(8, cols)], sem_in.at[0, j]),
            pltpu.make_async_copy(sc.at[j], scs.at[j, pl.ds(0, cols)], sem_in.at[1, j]),
            pltpu.make_async_copy(sd.at[j], sds.at[j, pl.ds(0, cols)], sem_in.at[2, j]),
            pltpu.make_async_copy(ec.at[j], ecs.at[j, pl.ds(0, cols)], sem_in.at[3, j]),
            pltpu.make_async_copy(ed.at[j], eds.at[j, pl.ds(0, cols)], sem_in.at[4, j]),
        )

    def start(j, c):
        for cp in copies(j):
            cp.start()
        return c

    lax.fori_loop(0, rows, start, 0)
    fx[1 : rows + 1, 7:8, :] = wf[...].reshape(rows, 1, lanes)
    fx[1 : rows + 1, cols + 8 : cols + 9, :] = ef[...].reshape(rows, 1, lanes)
    fx[0, 8 : cols + 8, :] = sf[...]
    fx[rows + 1, 8 : cols + 8, :] = nf[...]
    scs[rows, 0:cols, :] = nsc[...]
    sds[rows, 0:cols, :] = nsd[...]
    cps = copies(0)
    cps[0].wait()
    cps[1].wait()
    cps[2].wait()
    for o, n in CHUNKS:
        sx[0, o : o + n, :] = flux(
            scs[0, o : o + n, :] * keep,
            sds[0, o : o + n, :] * keep,
            fx[0, 8 + o : 8 + o + n, :],
            fx[1, 8 + o : 8 + o + n, :],
        )

    def body(j, c):
        @pl.when(j + 1 < rows)
        def _():
            nxt = copies(j + 1)
            nxt[0].wait()
            nxt[1].wait()
            nxt[2].wait()

        now = copies(j)
        now[3].wait()
        now[4].wait()
        ex[7:8, :] = flux(
            wec[pl.ds(j, 1), :], wed[pl.ds(j, 1), :], fx[j + 1, 7:8, :], fx[j + 1, 8:9, :]
        )
        slot = lax.rem(j, 2)
        for o, n in CHUNKS:
            ex[8 + o : 8 + o + n, :] = flux(
                ecs[j, o : o + n, :],
                eds[j, o : o + n, :],
                fx[j + 1, 8 + o : 8 + o + n, :],
                fx[j + 1, 9 + o : 9 + o + n, :],
            )
        for o, n in CHUNKS:
            here = fx[j + 1, 8 + o : 8 + o + n, :]
            north = flux(
                scs[j + 1, o : o + n, :],
                sds[j + 1, o : o + n, :],
                here,
                fx[j + 2, 8 + o : 8 + o + n, :],
            )
            sx[1 - slot, o : o + n, :] = north
            across = ex[8 + o : 8 + o + n, :] - ex[7 + o : 7 + o + n, :]
            ob[j, o : o + n, :] = here - across - (north - sx[slot, o : o + n, :])
        pltpu.make_async_copy(ob.at[j, pl.ds(0, cols)], out.at[j], sem_out.at[j]).start()
        return c

    lax.fori_loop(0, rows, body, 0)
    first_col[...] = ob[:, 0:1, :].reshape(rows, lanes)
    last_col[...] = ob[:, cols - 1 : cols, :].reshape(rows, lanes)
    first_row[...] = ob[0, 0:cols, :]
    last_row[...] = ob[rows - 1, 0:cols, :]

    def finish(j, c):
        pltpu.make_async_copy(ob.at[j, pl.ds(0, cols)], out.at[j], sem_out.at[j]).wait()
        return c

    lax.fori_loop(0, rows, finish, 0)


def substep(f, ec, ed, sc, sd, halos):
    rows, cols, lanes = f.shape
    hbm = pl.BlockSpec(memory_space=pl.ANY)
    vmem = pl.BlockSpec(memory_space=pltpu.VMEM)
    line = jax.ShapeDtypeStruct((rows, lanes), F32)
    row = jax.ShapeDtypeStruct((cols, lanes), F32)
    return pl.pallas_call(
        substep_kernel,
        out_shape=(jax.ShapeDtypeStruct(f.shape, F32), line, line, row, row),
        in_specs=[hbm] * 5 + [vmem] * 8,
        out_specs=(hbm, vmem, vmem, vmem, vmem),
        scratch_shapes=[
            pltpu.VMEM((rows + 2, 248, lanes), F32),
            pltpu.VMEM((rows, 232, lanes), F32),
            pltpu.VMEM((rows, 232, lanes), F32),
            pltpu.VMEM((rows + 1, 232, lanes), F32),
            pltpu.VMEM((rows + 1, 232, lanes), F32),
            pltpu.VMEM((248, lanes), F32),
            pltpu.VMEM((2, 232, lanes), F32),
            pltpu.VMEM((rows, 232, lanes), F32),
            pltpu.SemaphoreType.DMA((5, rows)),
            pltpu.SemaphoreType.DMA((rows,)),
        ],
        name="substep",
    )(f, ec, ed, sc, sd, *halos)


def tables():
    q = np.arange(NQ)
    angle = 2.0 * np.pi * ((q[:, None] * q[None, :]) % NQ) / NQ
    full = np.zeros((2 * OUTB, 2 * BLK))
    full[:NQ, :NQ] = np.cos(angle)
    full[:NQ, BLK : BLK + NQ] = np.sin(angle)
    full[OUTB : OUTB + NQ, :NQ] = -np.sin(angle)
    full[OUTB : OUTB + NQ, BLK : BLK + NQ] = np.cos(angle)
    bf = jnp.bfloat16.dtype
    high = full.astype(np.float32).astype(bf)
    low = (full - high.astype(np.float64)).astype(np.float32).astype(bf)
    twist = np.zeros((OUTB, 128), np.float32)
    for k in range(1, NK):
        phase = 2.0 * np.pi * ((q * k) % (NP * NQ)) / (NP * NQ)
        twist[:NQ, k] = np.cos(phase)
        twist[:NQ, 16 + k] = np.sin(phase)
    return high, low, twist


COS = [math.cos(math.pi * i / 8) for i in range(16)]
SIN = [math.sin(math.pi * i / 8) for i in range(16)]
HALF = math.sqrt(0.5)


def real_spectrum(x):
    a = [x[p] + x[p + 8] for p in range(8)]
    b = [x[p] - x[p + 8] for p in range(8)]
    c = [a[p] + a[p + 4] for p in range(4)]
    d = [a[p] - a[p + 4] for p in range(4)]
    re, im = [None] * NK, [None] * NK
    e0, e1 = c[0] + c[2], c[1] + c[3]
    re[0], re[8] = e0 + e1, e0 - e1
    re[4], im[4] = c[0] - c[2], c[3] - c[1]
    u, v = (d[1] - d[3]) * HALF, (d[1] + d[3]) * HALF
    re[2], im[2] = d[0] + u, -d[2] - v
    re[6], im[6] = d[0] - u, d[2] - v
    m = [None] + [b[p] - b[8 - p] for p in (1, 2, 3)]
    s = [None] + [b[p] + b[8 - p] for p in (1, 2, 3)]
    for k in (1, 3, 5, 7):
        real = b[0]
        imag = b[4] * (-SIN[4 * k % 16])
        for p in (1, 2, 3):
            real = real + m[p] * COS[p * k % 16]
            imag = imag - s[p] * SIN[p * k % 16]
        re[k], im[k] = real, imag
    return re, im


def real_values(re, im):
    y = [None] * NP
    even, odd = [None] * 8, [None] * 8
    plus, minus = re[0] + re[8], re[0] - re[8]
    f = [plus + re[4], minus - im[4], plus - re[4], minus + im[4]]
    r_sum, r_dif = re[2] + re[6], (re[2] - re[6]) * HALF
    i_sum, i_dif = (im[2] + im[6]) * HALF, im[6] - im[2]
    g = [r_sum, r_dif - i_sum, i_dif, -r_dif - i_sum]
    for p in range(4):
        even[p], even[p + 4] = f[p] + g[p], f[p] - g[p]
    odd[0] = re[1] + re[3] + re[5] + re[7]
    odd[4] = im[3] - im[1] + im[7] - im[5]
    for p in (1, 2, 3):
        cosine = re[1] * COS[p]
        sine = im[1] * SIN[p]
        for k in (3, 5, 7):
            cosine = cosine + re[k] * COS[p * k % 16]
            sine = sine + im[k] * SIN[p * k % 16]
        odd[p], odd[8 - p] = cosine - sine, -cosine - sine
    for p in range(8):
        y[p], y[p + 8] = even[p] + odd[p], even[p] - odd[p]
    return y


def split(value):
    high = value.astype(BF16)
    return high, (value - high.astype(F32)).astype(BF16)


TILES = tuple((o, 16) for o in range(0, 224, 16)) + ((224, 1),)


def filter_kernel(cut, x, high, low, twist, out, zh, zl, spec):
    length = NP * NQ
    lanes = x.shape[2]

    @pl.when(cut[0] >= length // 2)
    def _():
        out[...] = x[...]

    @pl.when(cut[0] < length // 2)
    def _():
        pad = jnp.zeros((16, NK * lanes), BF16)
        for base in (224, BLK + 224):
            zh[base : base + 16, :] = pad
            zl[base : base + 16, :] = pad

        def put(o, n, k, real, imag):
            sl = slice(k * lanes, (k + 1) * lanes)
            for base, value in ((0, real), (BLK, imag)):
                hi, lo = split(value)
                zh[base + o : base + o + n, sl] = hi
                zl[base + o : base + o + n, sl] = lo

        for o, n in TILES:
            re, im = real_spectrum([x[p, o : o + n, :] for p in range(NP)])
            for k in range(NK):
                if k == 0:
                    put(o, n, k, re[0], jnp.zeros_like(re[0]))
                    continue
                cosine = jnp.broadcast_to(twist[o : o + n, k : k + 1], (n, lanes))
                sine = jnp.broadcast_to(twist[o : o + n, 16 + k : 17 + k], (n, lanes))
                if k == 8:
                    put(o, n, k, re[8] * cosine, -(re[8] * sine))
                else:
                    put(
                        o, n, k,
                        re[k] * cosine + im[k] * sine,
                        im[k] * cosine - re[k] * sine,
                    )

        def product():
            for a in range(0, NK, 2):
                b = min(a + 2, NK)
                sl = slice(a * lanes, b * lanes)
                dot = functools.partial(jnp.dot, preferred_element_type=F32)
                spec[:, sl] = (
                    dot(low[...], zh[:, sl]) + dot(high[...], zl[:, sl]) + dot(high[...], zh[:, sl])
                )

        product()
        level = cut[0].astype(F32)
        for o, n in TILES:
            row = lax.broadcasted_iota(jnp.int32, (n, lanes), 0) + o
            for k in range(NK):
                wave = row * NP + k
                folded = jnp.minimum(wave, length - wave).astype(F32)
                ratio = level / jnp.maximum(folded, 1.0)
                scale = (1.0 if k in (0, 8) else 2.0) / length
                damping = jnp.minimum(1.0, ratio * ratio) * scale
                sl = slice(k * lanes, (k + 1) * lanes)
                put(
                    o, n, k,
                    spec[o : o + n, sl] * damping,
                    -(spec[OUTB + o : OUTB + o + n, sl] * damping),
                )
        product()
        for o, n in TILES:
            re, im = [None] * NK, [None] * NK
            for k in range(NK):
                sl = slice(k * lanes, (k + 1) * lanes)
                real = spec[o : o + n, sl]
                if k == 0:
                    re[0] = real
                    continue
                imag = spec[OUTB + o : OUTB + o + n, sl]
                cosine = jnp.broadcast_to(twist[o : o + n, k : k + 1], (n, lanes))
                sine = jnp.broadcast_to(twist[o : o + n, 16 + k : 17 + k], (n, lanes))
                re[k] = real * cosine + imag * sine
                if k < 8:
                    im[k] = real * sine - imag * cosine
            y = real_values(re, im)
            for p in range(NP):
                out[p, o : o + n, :] = y[p]


def filter_row(x, cut):
    high, low, twist = tables()
    lanes = x.shape[2]
    vmem = pl.BlockSpec(memory_space=pltpu.VMEM)
    return pl.pallas_call(
        filter_kernel,
        out_shape=jax.ShapeDtypeStruct(x.shape, F32),
        in_specs=[pl.BlockSpec(memory_space=pltpu.SMEM)] + [vmem] * 4,
        out_specs=vmem,
        scratch_shapes=[
            pltpu.VMEM((2 * BLK, NK * lanes), BF16),
            pltpu.VMEM((2 * BLK, NK * lanes), BF16),
            pltpu.VMEM((2 * OUTB, NK * lanes), F32),
        ],
        name="filter",
    )(cut, x, jnp.asarray(high), jnp.asarray(low), jnp.asarray(twist))


def moved(values, axis, step, periodic):
    count = lax.axis_size(axis)
    pairs = [(i, (i + step) % count) for i in range(count)]
    if not periodic:
        pairs = [(i, t) for i, t in pairs if t == i + step]
    return lax.ppermute(values, axis, pairs)


def on_device(tracer, ec, ed, sc, sd, cutoff):
    rows = tracer.shape[0]
    west = moved(jnp.stack([tracer[:, -1], ec[:, -1], ed[:, -1]]), "lon", 1, True)
    east = moved(tracer[:, 0], "lon", -1, True)
    north = moved(jnp.stack([tracer[0], sc[0], sd[0]]), "lat", -1, False)
    south = moved(tracer[-1], "lat", 1, False)
    wec, wed, nsc, nsd = west[1], west[2], north[1], north[2]
    field, c0, c1, r0, r1 = substep(
        tracer, ec, ed, sc, sd, (west[0], wec, wed, east, north[0], nsc, nsd, south)
    )
    west = moved(c1, "lon", 1, True)
    east = moved(c0, "lon", -1, True)
    north = moved(r0, "lat", -1, False)
    south = moved(r1, "lat", 1, False)
    field = substep(field, ec, ed, sc, sd, (west, wec, wed, east, north, nsc, nsd, south))[0]
    mine = lax.axis_index("lat") * rows + lax.axis_index("lon")
    cut = lax.dynamic_slice_in_dim(cutoff, mine, 1)
    whole = lax.all_to_all(field, "lon", split_axis=0, concat_axis=0, tiled=True)
    whole = filter_row(whole, cut)
    return lax.all_to_all(whole, "lon", split_axis=0, concat_axis=0, tiled=True)


def solution(mesh):
    spec = P("lat", "lon", None)
    return jax.shard_map(
        on_device, mesh=mesh, in_specs=(spec,) * 5 + (P(),), out_specs=spec, check_vma=False
    )
```

```python
import functools
import math

import jax
import jax.numpy as jnp
import numpy as np
from jax import lax
from jax.experimental import pallas as pl
from jax.experimental.pallas import tpu as pltpu
from jax.sharding import PartitionSpec as P

F32 = jnp.float32
BF16 = jnp.bfloat16
NP = 16
NQ = 225
NR = 16
BLK = 240
OUTB = 232
NK = 9
WEST = 4
EXT = NQ + WEST
LINE = 240
SHIFT = 2
STEP = 8


def even_lat():
    return lax.rem(lax.axis_index("lat"), 2) == 0


def message_kernel(f, ec, ed, sc, sd, west, line_a, corner_a, line_b, corner_b, tops, bots, scs, sds, sems):
    lanes = f.shape[2]
    fields = (f, ec, ed, sc, sd)
    columns = [
        pltpu.make_async_copy(x.at[pl.ds(NQ - WEST, WEST)], west.at[pl.ds(i * WEST, WEST)], sems.at[i])
        for i, x in enumerate(fields)
    ]
    lines = [
        pltpu.make_async_copy(f.at[:, pl.ds(8, 8), :], tops, sems.at[5]),
        pltpu.make_async_copy(f.at[:, pl.ds(0, 8), :], bots, sems.at[6]),
        pltpu.make_async_copy(sc.at[:, pl.ds(0, 8), :], scs, sems.at[7]),
        pltpu.make_async_copy(sd.at[:, pl.ds(0, 8), :], sds, sems.at[8]),
    ]
    for copy in lines + columns:
        copy.start()
    for copy in lines + columns:
        copy.wait()
    even = even_lat()
    for line in (line_a, line_b):
        line[:, 0:8, :] = jnp.zeros((2, 8, lanes), F32)
        line[:, 232:240, :] = jnp.zeros((2, 8, lanes), F32)
    for o in range(0, NQ, 8):
        n = min(8, NQ - o)
        half = 0.5 * scs[o : o + n, 0, :]
        mix = sds[o : o + n, 0, :]
        top = tops[o : o + n, 7, :]
        low, high = half + mix, (half - mix) * bots[o : o + n, 0, :]
        zero = jnp.zeros_like(top)
        sl = slice(8 + o, 8 + o + n)
        line_a[0, sl, :] = jnp.where(even, top, low)
        line_a[1, sl, :] = jnp.where(even, zero, high)
        line_b[0, sl, :] = jnp.where(even, low, top)
        line_b[1, sl, :] = jnp.where(even, high, zero)
    for line, corner in ((line_a, corner_a), (line_b, corner_b)):
        corner[:, 0:5, :] = jnp.zeros((2, 5, lanes), F32)
        corner[:, 5:8, :] = line[:, 8 + NQ - 3 : 8 + NQ, :]


def messages(f, ec, ed, sc, sd):
    lanes = f.shape[2]
    hbm = pl.BlockSpec(memory_space=pl.ANY)
    vmem = pl.BlockSpec(memory_space=pltpu.VMEM)
    line, corner = pltpu.VMEM((2, LINE, lanes), F32), pltpu.VMEM((2, 8, lanes), F32)
    return pl.pallas_call(
        message_kernel,
        out_shape=(pltpu.VMEM((5 * WEST, NR, lanes), F32), line, corner, line, corner),
        in_specs=[hbm] * 5,
        out_specs=(vmem,) * 5,
        scratch_shapes=[pltpu.VMEM((NQ, 8, lanes), F32)] * 4 + [pltpu.SemaphoreType.DMA((9,))],
        compiler_params=pltpu.CompilerParams(vmem_limit_bytes=12 << 20),
        name="messages",
    )(f, ec, ed, sc, sd)


def advance(f, ec, ed, sc, sd, before, south, north_low, north_high, keep):
    n = ec.shape[0]
    row = lax.broadcasted_iota(jnp.int32, (n, NR, f.shape[2]), 1)
    half = 0.5 * ec
    here = f[0:n]
    east = (half + ed) * here + (half - ed) * f[1 : n + 1]
    half = 0.5 * sc
    mask = jnp.where(row == 0, keep, 1.0)
    below = jnp.where(row == 0, south[:, None, :], pltpu.roll(here, 1, axis=1))
    low = (half - sd) * mask
    flux = (half + sd) * mask * below + low * here
    north_row = north_low[:, None, :] * here + north_high[:, None, :]
    north = jnp.where(row == NR - 1, north_row, pltpu.roll(flux, NR - 1, axis=1))
    previous = jnp.concatenate([before[None], east[: n - 1]], axis=0) if n > 1 else before[None]
    return here - (east - previous) - (north - flux), east[n - 1], low


def halo_lines(line_a, corner_a, line_b, corner_b, halo):
    even = even_lat()
    lanes = line_a.shape[2]

    def join(sl, a, b):
        halo[0, sl, :] = jnp.where(even, b[0], a[0])
        halo[1, sl, :] = jnp.where(even, a[0], b[0])
        halo[2, sl, :] = jnp.where(even, a[1], b[1])

    join(slice(0, 8), corner_a, corner_b)
    join(slice(8, LINE), line_a[:, 8:, :], line_b[:, 8:, :])


def first_kernel(f, ec, ed, sc, sd, west, la, ca, lb, cb, out, send_a, send_b, halo):
    lanes = f.shape[2]
    even = even_lat()
    keep = jnp.where(lax.axis_index("lat") > 0, 1.0, 0.0).astype(F32)
    halo_lines(la, ca, lb, cb, halo)
    for send in (send_a, send_b):
        send[0:8, :] = jnp.zeros((8, lanes), F32)
        send[232:240, :] = jnp.zeros((8, lanes), F32)

    def put(values, low, c, h, n):
        out[pl.ds(c, n)] = values
        top, bot = values[:, NR - 1, :], low[:, 0, :] * values[:, 0, :]
        send_a[pl.ds(h, n), :] = jnp.where(even, top, bot)
        send_b[pl.ds(h, n), :] = jnp.where(even, bot, top)

    w = [west[i * WEST : (i + 1) * WEST] for i in range(5)]
    half = 0.5 * w[1][0]
    before = (half + w[2][0]) * w[0][0] + (half - w[2][0]) * w[0][1]
    values, before, low = advance(
        jnp.concatenate([w[0][1:], f[0:1]], axis=0), w[1][1:], w[2][1:], w[3][1:], w[4][1:],
        before, halo[0, 5:8, :], halo[1, 5:8, :], halo[2, 5:8, :], keep,
    )
    put(values, low, 1, 5, 3)

    def body(i, before):
        q = i * STEP
        sl = pl.ds(q, STEP)
        h = pl.multiple_of(q + 8, 8)
        hs = pl.ds(h, STEP)
        values, last, low = advance(
            f[pl.ds(q, STEP + 1)], ec[sl], ed[sl], sc[sl], sd[sl], before,
            halo[0, hs, :], halo[1, hs, :], halo[2, hs, :], keep,
        )
        put(values, low, q + WEST, h, STEP)
        return last

    lax.fori_loop(0, (NQ - 1) // STEP, body, before)


def second_kernel(f1, ec, ed, sc, sd, west, la, ca, lb, cb, ra, rb, out, halo, cols, *, rows_out):
    lanes = f1.shape[2]
    even = even_lat()
    keep = jnp.where(lax.axis_index("lat") > 0, 1.0, 0.0).astype(F32)
    halo_lines(la, ca, lb, cb, halo)
    halo[0] = jnp.where(even, rb[...], ra[...])
    halo[2] = jnp.where(even, ra[...], rb[...])

    def put(values, s, n):
        if rows_out:
            cols[pl.ds(pl.multiple_of(s * NR, NR), n * NR), :] = values.reshape(n * NR, lanes)
        else:
            out[pl.ds(s, n)] = values

    w = [west[i * WEST : (i + 1) * WEST] for i in range(5)]
    half = 0.5 * w[1][1]
    before = (half + w[2][1]) * f1[1] + (half - w[2][1]) * f1[2]
    values, before, _ = advance(
        f1[2:5], w[1][2:], w[2][2:], w[3][2:], w[4][2:],
        before, halo[0, 6:8, :], halo[1, 6:8, :], halo[2, 6:8, :], keep,
    )
    put(values, 0, 2)

    def piece(q, n, h, before):
        sl = pl.ds(q, n)
        hs = pl.ds(h, n)
        values, last, _ = advance(
            f1[pl.ds(q + WEST, n + 1)], ec[sl], ed[sl], sc[sl], sd[sl], before,
            halo[0, hs, :], halo[1, hs, :], halo[2, hs, :], keep,
        )
        put(values, q + SHIFT, n)
        return last

    whole = (NQ - SHIFT) // STEP
    before = lax.fori_loop(
        0, whole, lambda i, b: piece(i * STEP, STEP, pl.multiple_of(i * STEP + 8, 8), b), before
    )
    q = whole * STEP
    piece(q, NQ - SHIFT - q, q + 8, before)
    if rows_out:

        def turn(i, c):
            for r in range(NR):
                out[r, pl.ds(pl.multiple_of(i * 8, 8), 8), :] = cols[
                    pl.ds(i * (8 * NR) + r, 8, stride=NR), :
                ]
            return c

        lax.fori_loop(0, NQ // 8, turn, 0)
        for r in range(NR):
            out[r, NQ - 1 : NQ, :] = cols[(NQ - 1) * NR + r : (NQ - 1) * NR + r + 1, :]


def pinned(x):
    return pltpu.with_memory_space_constraint(x, pltpu.VMEM)


def vmem_call(kernel, outs, scratch, name, args, smem=()):
    vmem = pl.BlockSpec(memory_space=pltpu.VMEM)
    single = not isinstance(outs, tuple)
    return pl.pallas_call(
        kernel,
        out_shape=outs,
        in_specs=[pl.BlockSpec(memory_space=pltpu.SMEM)] * len(smem) + [vmem] * len(args),
        out_specs=vmem if single else (vmem,) * len(outs),
        scratch_shapes=scratch,
        compiler_params=pltpu.CompilerParams(vmem_limit_bytes=12 << 20),
        name=name,
    )(*smem, *[pinned(x) for x in args])


def first_step(fields, west, halos):
    lanes = west.shape[2]
    line = pltpu.VMEM((LINE, lanes), F32)
    return vmem_call(
        first_kernel,
        (pltpu.VMEM((EXT, NR, lanes), F32), line, line),
        [pltpu.VMEM((3, LINE, lanes), F32)],
        "first", (*fields, west, *halos),
    )


def second_step(f1, fields, west, halos, rows_out):
    lanes = west.shape[2]
    shape = (NR, NQ, lanes) if rows_out else (NQ, NR, lanes)
    return vmem_call(
        functools.partial(second_kernel, rows_out=rows_out),
        pltpu.VMEM(shape, F32),
        [
            pltpu.VMEM((3, LINE, lanes), F32),
            pltpu.VMEM((NQ * NR if rows_out else 8, lanes), F32),
        ],
        "second", (f1, *fields[1:], west, *halos),
    )


def tables():
    q = np.arange(NQ)
    angle = 2.0 * np.pi * ((q[:, None] * q[None, :]) % NQ) / NQ
    full = np.zeros((2 * OUTB, 2 * BLK))
    full[:NQ, :NQ] = np.cos(angle)
    full[:NQ, BLK : BLK + NQ] = np.sin(angle)
    full[OUTB : OUTB + NQ, :NQ] = -np.sin(angle)
    full[OUTB : OUTB + NQ, BLK : BLK + NQ] = np.cos(angle)
    bf = jnp.bfloat16.dtype
    high = full.astype(np.float32).astype(bf)
    low = (full - high.astype(np.float64)).astype(np.float32).astype(bf)
    twist = np.zeros((OUTB, 128), np.float32)
    for k in range(1, NK):
        phase = 2.0 * np.pi * ((q * k) % (NP * NQ)) / (NP * NQ)
        twist[:NQ, k] = np.cos(phase)
        twist[:NQ, 16 + k] = np.sin(phase)
    return high, low, twist


COS = [math.cos(math.pi * i / 8) for i in range(16)]
SIN = [math.sin(math.pi * i / 8) for i in range(16)]
HALF = math.sqrt(0.5)


def real_spectrum(x):
    a = [x[p] + x[p + 8] for p in range(8)]
    b = [x[p] - x[p + 8] for p in range(8)]
    c = [a[p] + a[p + 4] for p in range(4)]
    d = [a[p] - a[p + 4] for p in range(4)]
    re, im = [None] * NK, [None] * NK
    e0, e1 = c[0] + c[2], c[1] + c[3]
    re[0], re[8] = e0 + e1, e0 - e1
    re[4], im[4] = c[0] - c[2], c[3] - c[1]
    u, v = (d[1] - d[3]) * HALF, (d[1] + d[3]) * HALF
    re[2], im[2] = d[0] + u, -d[2] - v
    re[6], im[6] = d[0] - u, d[2] - v
    m = [None] + [b[p] - b[8 - p] for p in (1, 2, 3)]
    s = [None] + [b[p] + b[8 - p] for p in (1, 2, 3)]
    for k in (1, 3, 5, 7):
        real = b[0]
        imag = b[4] * (-SIN[4 * k % 16])
        for p in (1, 2, 3):
            real = real + m[p] * COS[p * k % 16]
            imag = imag - s[p] * SIN[p * k % 16]
        re[k], im[k] = real, imag
    return re, im


def real_values(re, im):
    y = [None] * NP
    even, odd = [None] * 8, [None] * 8
    plus, minus = re[0] + re[8], re[0] - re[8]
    f = [plus + re[4], minus - im[4], plus - re[4], minus + im[4]]
    r_sum, r_dif = re[2] + re[6], (re[2] - re[6]) * HALF
    i_sum, i_dif = (im[2] + im[6]) * HALF, im[6] - im[2]
    g = [r_sum, r_dif - i_sum, i_dif, -r_dif - i_sum]
    for p in range(4):
        even[p], even[p + 4] = f[p] + g[p], f[p] - g[p]
    odd[0] = re[1] + re[3] + re[5] + re[7]
    odd[4] = im[3] - im[1] + im[7] - im[5]
    for p in (1, 2, 3):
        cosine = re[1] * COS[p]
        sine = im[1] * SIN[p]
        for k in (3, 5, 7):
            cosine = cosine + re[k] * COS[p * k % 16]
            sine = sine + im[k] * SIN[p * k % 16]
        odd[p], odd[8 - p] = cosine - sine, -cosine - sine
    for p in range(8):
        y[p], y[p + 8] = even[p] + odd[p], even[p] - odd[p]
    return y


def split(value):
    high = value.astype(BF16)
    return high, (value - high.astype(F32)).astype(BF16)


TILES = tuple((o, 16) for o in range(0, 224, 16)) + ((224, 1),)


def filter_kernel(cutoff, x, high, low, twist, out, zh, zl, spec):
    length = NP * NQ
    lanes = x.shape[2]
    cut = cutoff[lax.axis_index("lat") * NR + lax.axis_index("lon")]

    @pl.when(cut < length // 2)
    def _():
        pad = jnp.zeros((16, NK * lanes), BF16)
        for base in (224, BLK + 224):
            zh[base : base + 16, :] = pad
            zl[base : base + 16, :] = pad

        def put(o, n, k, real, imag):
            sl = slice(k * lanes, (k + 1) * lanes)
            for base, value in ((0, real), (BLK, imag)):
                hi, lo = split(value)
                zh[base + o : base + o + n, sl] = hi
                zl[base + o : base + o + n, sl] = lo

        for o, n in TILES:
            re, im = real_spectrum([x[p, o : o + n, :] for p in range(NP)])
            for k in range(NK):
                if k == 0:
                    put(o, n, k, re[0], jnp.zeros_like(re[0]))
                    continue
                cosine = jnp.broadcast_to(twist[o : o + n, k : k + 1], (n, lanes))
                sine = jnp.broadcast_to(twist[o : o + n, 16 + k : 17 + k], (n, lanes))
                if k == 8:
                    put(o, n, k, re[8] * cosine, -(re[8] * sine))
                else:
                    put(
                        o, n, k,
                        re[k] * cosine + im[k] * sine,
                        im[k] * cosine - re[k] * sine,
                    )

        def product():
            for a in range(0, NK, 2):
                b = min(a + 2, NK)
                sl = slice(a * lanes, b * lanes)
                dot = functools.partial(jnp.dot, preferred_element_type=F32)
                spec[:, sl] = (
                    dot(low[...], zh[:, sl]) + dot(high[...], zl[:, sl]) + dot(high[...], zh[:, sl])
                )

        product()
        level = cut.astype(F32)
        for o, n in TILES:
            row = lax.broadcasted_iota(jnp.int32, (n, lanes), 0) + o
            for k in range(NK):
                wave = row * NP + k
                folded = jnp.minimum(wave, length - wave).astype(F32)
                ratio = level / jnp.maximum(folded, 1.0)
                scale = (1.0 if k in (0, 8) else 2.0) / length
                damping = jnp.minimum(1.0, ratio * ratio) * scale
                sl = slice(k * lanes, (k + 1) * lanes)
                put(
                    o, n, k,
                    spec[o : o + n, sl] * damping,
                    -(spec[OUTB + o : OUTB + o + n, sl] * damping),
                )
        product()
        for o, n in TILES:
            re, im = [None] * NK, [None] * NK
            for k in range(NK):
                sl = slice(k * lanes, (k + 1) * lanes)
                real = spec[o : o + n, sl]
                if k == 0:
                    re[0] = real
                    continue
                imag = spec[OUTB + o : OUTB + o + n, sl]
                cosine = jnp.broadcast_to(twist[o : o + n, k : k + 1], (n, lanes))
                sine = jnp.broadcast_to(twist[o : o + n, 16 + k : 17 + k], (n, lanes))
                re[k] = real * cosine + imag * sine
                if k < 8:
                    im[k] = real * sine - imag * cosine
            y = real_values(re, im)
            for p in range(NP):
                if o == 0:
                    out[(p - 1) % NP, NQ - SHIFT : NQ, :] = y[p][:SHIFT]
                    out[p, 0 : n - SHIFT, :] = y[p][SHIFT:]
                else:
                    out[p, o - SHIFT : o - SHIFT + n, :] = y[p]


def filter_row(x, cutoff):
    lanes = x.shape[2]
    high, low, twist = (jnp.asarray(t) for t in tables())
    return vmem_call(
        filter_kernel,
        pltpu.VMEM(x.shape, F32),
        [
            pltpu.VMEM((2 * BLK, NK * lanes), BF16),
            pltpu.VMEM((2 * BLK, NK * lanes), BF16),
            pltpu.VMEM((2 * OUTB, NK * lanes), F32),
        ],
        "filter", (x, high, low, twist), (cutoff,),
    )


def join_kernel(cutoff, smooth, plain, edge, out):
    lanes = smooth.shape[2]
    first = lax.axis_index("lat") * NR
    out[0 : (NQ - SHIFT) * NR, :] = plain[SHIFT:NQ].reshape((NQ - SHIFT) * NR, lanes)
    out[(NQ - SHIFT) * NR : NQ * NR, :] = edge[...].reshape(SHIFT * NR, lanes)
    for r in range(NR):

        @pl.when(cutoff[first + r] < NP * NQ // 2)
        def _():
            for o in range(0, NQ - 1, 8):
                out[pl.ds(o * NR + r, 8, stride=NR), :] = smooth[r, o : o + 8, :]
            last = (NQ - 1) * NR + r
            out[last : last + 1, :] = smooth[r, NQ - 1 : NQ, :]


def join_rows(smooth, plain, edge, cutoff):
    lanes = smooth.shape[2]
    return vmem_call(
        join_kernel,
        jax.ShapeDtypeStruct((NQ * NR, lanes), F32),
        [],
        "join", (smooth, plain, edge), (cutoff,),
    ).reshape(NQ, NR, lanes)


def pairs_of(kind, shift):
    count, across = lax.axis_size("lat"), lax.axis_size("lon")
    out = []
    for lat in range(count):
        other = lat ^ 1 if kind == "a" else ((lat + 1) ^ 1) - 1
        if 0 <= other < count:
            out += [(lat * across + p, other * across + (p + shift) % across) for p in range(across)]
    return out


def moved(values, kind, shift=0):
    return lax.ppermute(values, ("lat", "lon"), pairs_of(kind, shift))


def round_lon(values, step):
    count = lax.axis_size("lon")
    return lax.ppermute(values, "lon", [(i, (i + step) % count) for i in range(count)])


def on_device(tracer, ec, ed, sc, sd, cutoff):
    fields = tuple(jnp.transpose(x, (1, 0, 2)) for x in (tracer, ec, ed, sc, sd))
    west, line_a, corner_a, line_b, corner_b = messages(*fields)
    west = round_lon(west, 1)
    got_corner_a = moved(corner_a, "a", 1)
    got_line_a = moved(line_a, "a")
    none_line, none_corner = jnp.zeros_like(line_b), jnp.zeros_like(corner_b)
    halos = (got_line_a, got_corner_a, none_line, none_corner)
    f1, send_a, _ = first_step(fields, west, halos)
    got_a = moved(send_a, "a")
    rows = second_step(f1, fields, west, (*halos, got_a, jnp.zeros_like(got_a)), True)
    rows, line_b, corner_b = lax.optimization_barrier((rows, line_b, corner_b))
    whole = lax.all_to_all(rows, "lon", split_axis=0, concat_axis=0, tiled=True)
    halos = (got_line_a, got_corner_a, moved(line_b, "b"), moved(corner_b, "b", 1))
    f1, send_a, send_b = first_step(fields, west, halos)
    plain = second_step(f1, fields, west, (*halos, moved(send_a, "a"), moved(send_b, "b")), False)
    edge = round_lon(plain[:SHIFT], -1)
    whole = filter_row(whole, cutoff)
    smooth = lax.all_to_all(whole, "lon", split_axis=0, concat_axis=0, tiled=True)
    return jnp.transpose(join_rows(smooth, plain, edge, cutoff), (1, 0, 2))


def solution(mesh):
    spec = P("lat", "lon", None)
    return jax.shard_map(
        on_device, mesh=mesh, in_specs=(spec,) * 5 + (P(),), out_specs=spec, check_vma=False
    )
```

```python
import functools
import math

import jax
import jax.numpy as jnp
import numpy as np
from jax import lax
from jax.experimental import pallas as pl
from jax.experimental.pallas import tpu as pltpu
from jax.sharding import PartitionSpec as P

F32 = jnp.float32
BF16 = jnp.bfloat16
NP = 16
NQ = 225
NR = 16
BLK = 240
OUTB = 232
NK = 9
WEST = 4
EXT = NQ + WEST
LINE = 240
SHIFT = 2
STEP = 8


def keep_south():
    return jnp.where(lax.axis_index("lat") > 0, 1.0, 0.0).astype(F32)


def even_lat():
    return lax.rem(lax.axis_index("lat"), 2) == 0


def message_kernel(
    f, ec, ed, sc, sd, west, line_a, line_b, top, low, high, tops, bots, scs, sds, sems
):
    lanes = f.shape[2]
    fields = (f, ec, ed, sc, sd)
    columns = [
        pltpu.make_async_copy(x.at[pl.ds(NQ - WEST, WEST)], west.at[pl.ds(i * WEST, WEST)], sems.at[i])
        for i, x in enumerate(fields)
    ]
    lines = [
        pltpu.make_async_copy(f.at[:, pl.ds(8, 8), :], tops, sems.at[5]),
        pltpu.make_async_copy(f.at[:, pl.ds(0, 8), :], bots, sems.at[6]),
        pltpu.make_async_copy(sc.at[:, pl.ds(0, 8), :], scs, sems.at[7]),
        pltpu.make_async_copy(sd.at[:, pl.ds(0, 8), :], sds, sems.at[8]),
    ]
    for copy in lines + columns:
        copy.start()
    even, keep = even_lat(), keep_south()
    zero = jnp.zeros((8, lanes), F32)
    for line in (top, low, high, line_a.at[0], line_a.at[1], line_b.at[0], line_b.at[1]):
        line[0:8, :] = zero
        line[232:240, :] = zero
    for copy in lines:
        copy.wait()
    for o in range(0, NQ, 8):
        n = min(8, NQ - o)
        half = 0.5 * scs[o : o + n, 0, :]
        mix = sds[o : o + n, 0, :]
        north = tops[o : o + n, 7, :]
        a, b = (half + mix) * keep, (half - mix) * keep
        term = b * bots[o : o + n, 0, :]
        sl = slice(8 + o, 8 + o + n)
        top[sl, :], low[sl, :], high[sl, :] = north, a, b
        line_a[0, sl, :] = jnp.where(even, north, a)
        line_a[1, sl, :] = jnp.where(even, 0.0, term)
        line_b[0, sl, :] = jnp.where(even, a, north)
        line_b[1, sl, :] = jnp.where(even, term, 0.0)
    for copy in columns:
        copy.wait()


def messages(f, ec, ed, sc, sd):
    lanes = f.shape[2]
    hbm = pl.BlockSpec(memory_space=pl.ANY)
    vmem = pl.BlockSpec(memory_space=pltpu.VMEM)
    double, line = pltpu.VMEM((2, LINE, lanes), F32), pltpu.VMEM((LINE, lanes), F32)
    return pl.pallas_call(
        message_kernel,
        out_shape=(pltpu.VMEM((5 * WEST, NR, lanes), F32), double, double, line, line, line),
        in_specs=[hbm] * 5,
        out_specs=(vmem,) * 6,
        scratch_shapes=[pltpu.VMEM((NQ, 8, lanes), F32)] * 4 + [pltpu.SemaphoreType.DMA((9,))],
        compiler_params=pltpu.CompilerParams(vmem_limit_bytes=12 << 20),
        name="messages",
    )(*[pltpu.with_memory_space_constraint(x, pltpu.HBM) for x in (f, ec, ed, sc, sd)])


def advance(f, ec, ed, sc, sd, before, keep):
    n = ec.shape[0]
    row = lax.broadcasted_iota(jnp.int32, (n, NR, f.shape[2]), 1)
    half = 0.5 * ec
    here = f[0:n]
    east = (half + ed) * here + (half - ed) * f[1 : n + 1]
    half = 0.5 * sc
    edge = row == 0
    below = jnp.where(edge, 0.0, pltpu.roll(here, 1, axis=1))
    flux = (half + sd) * below + (half - sd) * jnp.where(edge, keep, 1.0) * here
    north = jnp.where(row == NR - 1, 0.0, pltpu.roll(flux, NR - 1, axis=1))
    previous = jnp.concatenate([before[None], east[: n - 1]], axis=0) if n > 1 else before[None]
    return here - (east - previous) - (north - flux), east[n - 1]


def first_kernel(f, ec, ed, sc, sd, out, bottom, upper):
    keep = keep_south()
    lanes = f.shape[2]

    def body(i, before):
        q = i * STEP
        sl = pl.ds(q, STEP)
        values, last = advance(f[pl.ds(q, STEP + 1)], ec[sl], ed[sl], sc[sl], sd[sl], before, keep)
        out[sl] = values
        hs = pl.ds(pl.multiple_of(q + 8, 8), STEP)
        bottom[hs, :] = values[:, 0, :]
        upper[hs, :] = values[:, NR - 1, :]
        return last

    lax.fori_loop(0, (NQ - 1) // STEP, body, jnp.zeros((NR, lanes), F32))


def pack_kernel(columns, line_a, line_b, out):
    even = even_lat()
    out[0 : 5 * WEST] = columns[...]
    sl = slice(8 + NQ - 3, 8 + NQ)
    a, b = line_a[:, sl, :], line_b[:, sl, :]
    out[5 * WEST, 0:3, :] = jnp.where(even, b[0], a[0])
    out[5 * WEST, 3:6, :] = jnp.where(even, a[0], b[0])
    out[5 * WEST, 6:9, :] = jnp.where(even, a[1], b[1])
    out[5 * WEST, 9:16, :] = jnp.zeros((7, columns.shape[2]), F32)


def repair_kernel(
    f1, bottom, upper, top, low, high, line_a, line_b, west, f,
    ext, row_low, row_high, face_low, face_high, send_a, send_b,
):
    even, keep = even_lat(), keep_south()
    lanes = f1.shape[2]
    w = [west[i * WEST : (i + 1) * WEST] for i in range(5)]
    corner = west[5 * WEST]
    half = 0.5 * w[1][0]
    before = (half + w[2][0]) * w[0][0] + (half - w[2][0]) * w[0][1]
    values, before = advance(
        jnp.concatenate([w[0][1:], f[0:1]], axis=0), w[1][1:], w[2][1:], w[3][1:], w[4][1:],
        before, keep,
    )
    first = f1[0] + before
    half, mix = 0.5 * w[3][1:, 0, :], w[4][1:, 0, :]
    a, b = (half + mix) * keep, (half - mix) * keep
    added = a * corner[0:3]
    taken = corner[3:6] * w[0][1:, NR - 1, :] + corner[6:9]
    south, north = values[:, 0, :] + added, values[:, NR - 1, :] - taken
    zero = jnp.zeros((8, lanes), F32)
    for line in (row_low, row_high, face_low, face_high, send_a, send_b):
        line[0:8, :] = zero
        line[232:240, :] = zero

    def put(sl, south, north, a, b, face):
        row_low[sl, :], row_high[sl, :] = south, north
        face_low[sl, :], face_high[sl, :] = a, face
        send_a[sl, :] = jnp.where(even, north, b * south)
        send_b[sl, :] = jnp.where(even, b * south, north)

    put(slice(5, 8), south, north, a, b, corner[3:6])
    for o in range(8, 232, 8):
        sl = slice(o, o + 8)
        outer_south = jnp.where(even, line_b[0, sl, :], line_a[0, sl, :])
        face = jnp.where(even, line_a[0, sl, :], line_b[0, sl, :])
        term = jnp.where(even, line_a[1, sl, :], line_b[1, sl, :])
        base_low, base_high = bottom[sl, :], upper[sl, :]
        if o == 8:
            base_low = jnp.concatenate([first[0:1], base_low[1:]], axis=0)
            base_high = jnp.concatenate([first[NR - 1 :], base_high[1:]], axis=0)
        put(
            sl,
            base_low + low[sl, :] * outer_south,
            base_high - (face * top[sl, :] + term),
            low[sl, :], high[sl, :], face,
        )
    ext[0:3] = values
    ext[3] = first


def second_kernel(f1, ec, ed, sc, sd, west, ext, row_low, row_high, out, cols):
    lanes = f1.shape[2]
    keep = keep_south()

    def whole(values, h, n):
        row = lax.broadcasted_iota(jnp.int32, (n, NR, lanes), 1)
        south, north = row_low[pl.ds(h, n), :], row_high[pl.ds(h, n), :]
        return jnp.where(
            row == 0, south[:, None, :], jnp.where(row == NR - 1, north[:, None, :], values)
        )

    def put(values, s, n):
        cols[pl.ds(pl.multiple_of(s * NR, NR), n * NR), :] = values.reshape(n * NR, lanes)

    w = [west[i * WEST : (i + 1) * WEST] for i in range(5)]
    near = whole(ext[...], 5, 4)
    half = 0.5 * w[1][1]
    before = (half + w[2][1]) * near[0] + (half - w[2][1]) * near[1]
    values, before = advance(near[1:], w[1][2:], w[2][2:], w[3][2:], w[4][2:], before, keep)
    put(values, 0, 2)

    def piece(q, n, h, before, lead=None):
        sl = pl.ds(q, n)
        field = f1[pl.ds(q, n + 1)] if lead is None else jnp.concatenate([lead, f1[1 : n + 1]], axis=0)
        values, last = advance(whole(field, h, n + 1), ec[sl], ed[sl], sc[sl], sd[sl], before, keep)
        put(values, q + SHIFT, n)
        return last

    before = piece(0, STEP, 8, before, ext[3:4])
    count = (NQ - SHIFT) // STEP
    before = lax.fori_loop(
        1, count, lambda i, b: piece(i * STEP, STEP, pl.multiple_of(i * STEP + 8, 8), b), before
    )
    q = count * STEP
    piece(q, NQ - SHIFT - q, q + 8, before)

    def turn(i, c):
        for r in range(NR):
            out[r, pl.ds(pl.multiple_of(i * 8, 8), 8), :] = cols[
                pl.ds(i * (8 * NR) + r, 8, stride=NR), :
            ]
        return c

    lax.fori_loop(0, NQ // 8, turn, 0)
    for r in range(NR):
        out[r, NQ - 1 : NQ, :] = cols[(NQ - 1) * NR + r : (NQ - 1) * NR + r + 1, :]


def finish_kernel(rows, row_high, face_low, face_high, send_a, send_b, out):
    even = even_lat()
    for s in range(0, NQ, 8):
        n = min(8, NQ - s)
        sl, hs = slice(s, s + n), slice(s + 8 - SHIFT, s + 8 - SHIFT + n)
        a, b = send_a[hs, :], send_b[hs, :]
        out[0, sl, :] = rows[0, sl, :] + face_low[hs, :] * jnp.where(even, b, a)
        out[NR - 1, sl, :] = rows[NR - 1, sl, :] - (
            face_high[hs, :] * row_high[hs, :] + jnp.where(even, a, b)
        )


def pinned(x):
    return pltpu.with_memory_space_constraint(x, pltpu.VMEM)


def vmem_call(kernel, outs, scratch, name, args, smem=(), alias=None):
    vmem = pl.BlockSpec(memory_space=pltpu.VMEM)
    single = not isinstance(outs, tuple)
    return pl.pallas_call(
        kernel,
        out_shape=outs,
        in_specs=[pl.BlockSpec(memory_space=pltpu.SMEM)] * len(smem) + [vmem] * len(args),
        out_specs=vmem if single else (vmem,) * len(outs),
        scratch_shapes=scratch,
        input_output_aliases=alias or {},
        compiler_params=pltpu.CompilerParams(vmem_limit_bytes=12 << 20),
        name=name,
    )(*smem, *[pinned(x) for x in args])


def tables():
    q = np.arange(NQ)
    angle = 2.0 * np.pi * ((q[:, None] * q[None, :]) % NQ) / NQ
    full = np.zeros((2 * OUTB, 2 * BLK))
    full[:NQ, :NQ] = np.cos(angle)
    full[:NQ, BLK : BLK + NQ] = np.sin(angle)
    full[OUTB : OUTB + NQ, :NQ] = -np.sin(angle)
    full[OUTB : OUTB + NQ, BLK : BLK + NQ] = np.cos(angle)
    bf = jnp.bfloat16.dtype
    high = full.astype(np.float32).astype(bf)
    low = (full - high.astype(np.float64)).astype(np.float32).astype(bf)
    twist = np.zeros((OUTB, 128), np.float32)
    for k in range(1, NK):
        phase = 2.0 * np.pi * ((q * k) % (NP * NQ)) / (NP * NQ)
        twist[:NQ, k] = np.cos(phase)
        twist[:NQ, 16 + k] = np.sin(phase)
    return high, low, twist


COS = [math.cos(math.pi * i / 8) for i in range(16)]
SIN = [math.sin(math.pi * i / 8) for i in range(16)]
HALF = math.sqrt(0.5)


def real_spectrum(x):
    a = [x[p] + x[p + 8] for p in range(8)]
    b = [x[p] - x[p + 8] for p in range(8)]
    c = [a[p] + a[p + 4] for p in range(4)]
    d = [a[p] - a[p + 4] for p in range(4)]
    re, im = [None] * NK, [None] * NK
    e0, e1 = c[0] + c[2], c[1] + c[3]
    re[0], re[8] = e0 + e1, e0 - e1
    re[4], im[4] = c[0] - c[2], c[3] - c[1]
    u, v = (d[1] - d[3]) * HALF, (d[1] + d[3]) * HALF
    re[2], im[2] = d[0] + u, -d[2] - v
    re[6], im[6] = d[0] - u, d[2] - v
    m = [None] + [b[p] - b[8 - p] for p in (1, 2, 3)]
    s = [None] + [b[p] + b[8 - p] for p in (1, 2, 3)]
    for k in (1, 3, 5, 7):
        real = b[0]
        imag = b[4] * (-SIN[4 * k % 16])
        for p in (1, 2, 3):
            real = real + m[p] * COS[p * k % 16]
            imag = imag - s[p] * SIN[p * k % 16]
        re[k], im[k] = real, imag
    return re, im


def real_values(re, im):
    y = [None] * NP
    even, odd = [None] * 8, [None] * 8
    plus, minus = re[0] + re[8], re[0] - re[8]
    f = [plus + re[4], minus - im[4], plus - re[4], minus + im[4]]
    r_sum, r_dif = re[2] + re[6], (re[2] - re[6]) * HALF
    i_sum, i_dif = (im[2] + im[6]) * HALF, im[6] - im[2]
    g = [r_sum, r_dif - i_sum, i_dif, -r_dif - i_sum]
    for p in range(4):
        even[p], even[p + 4] = f[p] + g[p], f[p] - g[p]
    odd[0] = re[1] + re[3] + re[5] + re[7]
    odd[4] = im[3] - im[1] + im[7] - im[5]
    for p in (1, 2, 3):
        cosine = re[1] * COS[p]
        sine = im[1] * SIN[p]
        for k in (3, 5, 7):
            cosine = cosine + re[k] * COS[p * k % 16]
            sine = sine + im[k] * SIN[p * k % 16]
        odd[p], odd[8 - p] = cosine - sine, -cosine - sine
    for p in range(8):
        y[p], y[p + 8] = even[p] + odd[p], even[p] - odd[p]
    return y


def split(value):
    high = value.astype(BF16)
    return high, (value - high.astype(F32)).astype(BF16)


TILES = tuple((o, 16) for o in range(0, 224, 16)) + ((224, 1),)


def unshift(out, p, o, n, value):
    if o == 0:
        out[(p - 1) % NP, NQ - SHIFT : NQ, :] = value[:SHIFT]
        out[p, 0 : n - SHIFT, :] = value[SHIFT:]
    else:
        out[p, o - SHIFT : o - SHIFT + n, :] = value


def filter_kernel(cutoff, x, high, low, twist, out, zh, zl, spec):
    length = NP * NQ
    lanes = x.shape[2]
    cut = cutoff[lax.axis_index("lat") * NR + lax.axis_index("lon")]

    @pl.when(cut >= length // 2)
    def _():
        for p in range(NP):
            for o, n in TILES:
                unshift(out, p, o, n, x[p, o : o + n, :])

    @pl.when(cut < length // 2)
    def _():
        pad = jnp.zeros((16, NK * lanes), BF16)
        for base in (224, BLK + 224):
            zh[base : base + 16, :] = pad
            zl[base : base + 16, :] = pad

        def put(o, n, k, real, imag):
            sl = slice(k * lanes, (k + 1) * lanes)
            for base, value in ((0, real), (BLK, imag)):
                hi, lo = split(value)
                zh[base + o : base + o + n, sl] = hi
                zl[base + o : base + o + n, sl] = lo

        for o, n in TILES:
            re, im = real_spectrum([x[p, o : o + n, :] for p in range(NP)])
            for k in range(NK):
                if k == 0:
                    put(o, n, k, re[0], jnp.zeros_like(re[0]))
                    continue
                cosine = jnp.broadcast_to(twist[o : o + n, k : k + 1], (n, lanes))
                sine = jnp.broadcast_to(twist[o : o + n, 16 + k : 17 + k], (n, lanes))
                if k == 8:
                    put(o, n, k, re[8] * cosine, -(re[8] * sine))
                else:
                    put(
                        o, n, k,
                        re[k] * cosine + im[k] * sine,
                        im[k] * cosine - re[k] * sine,
                    )

        def product():
            for a in range(0, NK, 2):
                b = min(a + 2, NK)
                sl = slice(a * lanes, b * lanes)
                dot = functools.partial(jnp.dot, preferred_element_type=F32)
                spec[:, sl] = (
                    dot(low[...], zh[:, sl]) + dot(high[...], zl[:, sl]) + dot(high[...], zh[:, sl])
                )

        product()
        level = cut.astype(F32)
        for o, n in TILES:
            row = lax.broadcasted_iota(jnp.int32, (n, lanes), 0) + o
            for k in range(NK):
                wave = row * NP + k
                folded = jnp.minimum(wave, length - wave).astype(F32)
                ratio = level / jnp.maximum(folded, 1.0)
                scale = (1.0 if k in (0, 8) else 2.0) / length
                damping = jnp.minimum(1.0, ratio * ratio) * scale
                sl = slice(k * lanes, (k + 1) * lanes)
                put(
                    o, n, k,
                    spec[o : o + n, sl] * damping,
                    -(spec[OUTB + o : OUTB + o + n, sl] * damping),
                )
        product()
        for o, n in TILES:
            re, im = [None] * NK, [None] * NK
            for k in range(NK):
                sl = slice(k * lanes, (k + 1) * lanes)
                real = spec[o : o + n, sl]
                if k == 0:
                    re[0] = real
                    continue
                imag = spec[OUTB + o : OUTB + o + n, sl]
                cosine = jnp.broadcast_to(twist[o : o + n, k : k + 1], (n, lanes))
                sine = jnp.broadcast_to(twist[o : o + n, 16 + k : 17 + k], (n, lanes))
                re[k] = real * cosine + imag * sine
                if k < 8:
                    im[k] = real * sine - imag * cosine
            y = real_values(re, im)
            for p in range(NP):
                unshift(out, p, o, n, y[p])


def filter_row(x, cutoff):
    lanes = x.shape[2]
    high, low, twist = (jnp.asarray(t) for t in tables())
    return vmem_call(
        filter_kernel,
        pltpu.VMEM(x.shape, F32),
        [
            pltpu.VMEM((2 * BLK, NK * lanes), BF16),
            pltpu.VMEM((2 * BLK, NK * lanes), BF16),
            pltpu.VMEM((2 * OUTB, NK * lanes), F32),
        ],
        "filter", (x, high, low, twist), (cutoff,),
    )


JOIN = ((0, 56), (56, 56), (112, 56), (168, 57))


def join_kernel(x, out, buf, sems):
    copies = []
    for i, (o, n) in enumerate(JOIN):

        def turn(t, c):
            q = pl.multiple_of(o + t * 8, 8)
            for r in range(NR):
                buf[pl.ds(q * NR + r, 8, stride=NR), :] = x[r, pl.ds(q, 8), :]
            return c

        lax.fori_loop(0, n // 8, turn, 0)
        if n % 8:
            q = NQ - 1
            for r in range(NR):
                buf[q * NR + r : q * NR + r + 1, :] = x[r, q : q + 1, :]
        part = pl.ds(o * NR, n * NR)
        copy = pltpu.make_async_copy(buf.at[part], out.at[part], sems.at[i])
        copy.start()
        copies.append(copy)
    for copy in copies:
        copy.wait()


def join_rows(x):
    lanes = x.shape[2]
    return pl.pallas_call(
        join_kernel,
        out_shape=jax.ShapeDtypeStruct((NQ * NR, lanes), F32),
        in_specs=[pl.BlockSpec(memory_space=pltpu.VMEM)],
        out_specs=pl.BlockSpec(memory_space=pl.ANY),
        scratch_shapes=[pltpu.VMEM((NQ * NR, lanes), F32), pltpu.SemaphoreType.DMA((len(JOIN),))],
        compiler_params=pltpu.CompilerParams(vmem_limit_bytes=12 << 20),
        name="join",
    )(pinned(x)).reshape(NQ, NR, lanes)


def pairs_of(kind, shift):
    count, across = lax.axis_size("lat"), lax.axis_size("lon")
    out = []
    for lat in range(count):
        other = lat ^ 1 if kind == "a" else ((lat + 1) ^ 1) - 1
        if 0 <= other < count:
            out += [(lat * across + p, other * across + (p + shift) % across) for p in range(across)]
    return out


def moved(values, kind, shift=0):
    return lax.ppermute(values, ("lat", "lon"), pairs_of(kind, shift))


def round_lon(values, step):
    count = lax.axis_size("lon")
    return lax.ppermute(values, "lon", [(i, (i + step) % count) for i in range(count)])


def on_device(tracer, ec, ed, sc, sd, cutoff):
    fields = tuple(jnp.transpose(x, (1, 0, 2)) for x in (tracer, ec, ed, sc, sd))
    lanes = tracer.shape[2]
    line, box = pltpu.VMEM((LINE, lanes), F32), pltpu.VMEM((NQ, NR, lanes), F32)
    columns, line_a, line_b, top, low, high = messages(*fields)
    columns, line_a, line_b, fields = lax.optimization_barrier((columns, line_a, line_b, fields))
    line_a, line_b = moved(line_a, "a"), moved(line_b, "b")
    f1, bottom, upper = vmem_call(first_kernel, (box, line, line), [], "first", fields)
    west = vmem_call(
        pack_kernel, pltpu.VMEM((5 * WEST + 1, NR, lanes), F32), [], "pack",
        (columns, line_a, line_b),
    )
    west = round_lon(west, 1)
    ext, row_low, row_high, face_low, face_high, send_a, send_b = vmem_call(
        repair_kernel, (pltpu.VMEM((WEST, NR, lanes), F32),) + (line,) * 6, [], "repair",
        (f1, bottom, upper, top, low, high, line_a, line_b, west, fields[0]),
    )
    send_a, send_b = moved(send_a, "a"), moved(send_b, "b")
    rows = vmem_call(
        second_kernel, pltpu.VMEM((NR, NQ, lanes), F32), [pltpu.VMEM((NQ * NR, lanes), F32)],
        "second", (f1, *fields[1:], west, ext, row_low, row_high),
    )
    rows = vmem_call(
        finish_kernel, pltpu.VMEM((NR, NQ, lanes), F32), [], "finish",
        (rows, row_high, face_low, face_high, send_a, send_b), alias={0: 0},
    )
    whole = lax.all_to_all(rows, "lon", split_axis=0, concat_axis=0, tiled=True)
    whole = filter_row(whole, cutoff)
    rows = lax.all_to_all(whole, "lon", split_axis=0, concat_axis=0, tiled=True)
    return jnp.transpose(join_rows(rows), (1, 0, 2))


def solution(mesh):
    spec = P("lat", "lon", None)
    return jax.shard_map(
        on_device, mesh=mesh, in_specs=(spec,) * 5 + (P(),), out_specs=spec, check_vma=False
    )
```
